32 devices in a mesh: groups: 2 (over y), seq: 8 (over z, x), head: 2 (over core).
Axes of the slice: x: 2, y: 2, z: 4, core: 2. Of those that a mesh axis runs over, the one named last changes fastest.
Arguments:
- big_queries: bfloat16 [512, 4096], P(('groups', 'seq'), 'head'), parts along dimension 0, may hold values from -160 to 160
- big_keys: bfloat16 [512, 4096], P(('groups', 'seq'), 'head'), parts along dimension 0, may hold values from -8 to 8
- big_values: bfloat16 [512, 4096], P(('groups', 'seq'), 'head'), parts along dimension 0, may hold values from -6 to 6
- small_queries: bfloat16 [512, 1024], P(('groups', 'seq', 'head')), parts along dimension 0, may hold values from -160 to 160
- small_keys: bfloat16 [512, 1024], P(('groups', 'seq', 'head')), parts along dimension 0, may hold values from -8 to 8
- small_values: bfloat16 [512, 1024], P(('groups', 'seq', 'head')), parts along dimension 0, may hold values from -6 to 6
- big_readout: bfloat16 [4096, 64], P('head'), may hold values from -0.75 to 0.75
- small_readout: bfloat16 [1024, 64], replicated, may hold values from -1.5 to 1.5
- guidance: float32 [2], P('groups'), parts along dimension 0, may hold values from 1 to 4
Outputs:
- guided: float32 [256, 128], P(('groups', 'seq')), parts along dimension 0
The draws below stay inside these ranges and needn't reach their ends.
There are 2 independent parts, one for each index of `groups`. The reference program is written for one: setup_inputs(seed, part) draws one part's arguments, and reference() takes and returns one part's arrays. A program takes and returns all parts, laid end to end along the dimension named above; an argument that names none is the same for every part. Nothing has to cross between parts.
All inputs are finite; a program needn't handle non-finite values.
Results may differ from the reference program's by a relative error of at most 0.0035.
Values may be sent and summed in bfloat16 or wider, within the bound.
A program may use at most 64 MiB of HBM per device.

```python
import math
import jax
import jax.numpy as jnp
from jax import lax

DH = 128
HB = 32
HS = 8
LAT = 64
TOKENS = 256


def paired(key, heads, salt):
    folded = jax.random.fold_in(key, salt)
    query_seed, key_seed = jax.random.split(folded, 2)
    extent = (TOKENS, heads, DH)
    query_draw = jnp.clip(1.41 * jax.random.normal(query_seed, extent, jnp.float32), -8.0, 8.0)
    key_draw = jnp.clip(1.41 * jax.random.normal(key_seed, extent, jnp.float32), -8.0, 8.0)
    return (query_draw.reshape(TOKENS, heads * DH), key_draw.reshape(TOKENS, heads * DH))


def draw_big_queries(key, part):
    return paired(key, HB, 101)[0].astype(jnp.bfloat16)


def draw_big_keys(key, part):
    return paired(key, HB, 101)[1].astype(jnp.bfloat16)


def draw_small_queries(key, part):
    return paired(key, HS, 202)[0].astype(jnp.bfloat16)


def draw_small_keys(key, part):
    return paired(key, HS, 202)[1].astype(jnp.bfloat16)


def shard_levels(key, shape, cuts, least, top_value):
    def one(dim, shards_of):
        draws = jax.random.uniform(jax.random.fold_in(jax.random.fold_in(key, 6), dim), (shards_of,), jnp.float32, least / len(cuts), top_value / len(cuts))
        return jnp.repeat(jnp.exp(draws), shape[dim] // shards_of).reshape((-1,) + (1,) * (len(shape) - dim - 1))

    factor_of = one(*cuts[0])
    for cut in cuts[1:]:
        factor_of = factor_of * one(*cut)
    return factor_of


def gaussian(stream_key, dims, scale, limit, pieces=(), held_as=jnp.bfloat16):
    array = scale * jax.random.normal(stream_key, dims, jnp.float32)
    if pieces:
        array = array * shard_levels(stream_key, dims, pieces, -0.22, 0.18)
    return jnp.clip(array, -limit, limit).astype(held_as)


def setup_inputs(seed: int = 0, part: int = 0) -> dict:
    splits = jax.random.split(jax.random.key(seed), 10)
    part_keys = jax.random.split(jax.random.fold_in(splits[9], part), 10)
    big_queries = draw_big_queries(jax.random.fold_in(jax.random.fold_in(splits[9], part), 71), part)
    big_keys = draw_big_keys(jax.random.fold_in(jax.random.fold_in(splits[9], part), 71), part)
    big_values = gaussian(part_keys[2], (TOKENS, HB * DH), 1.0, 6.0, ((0, 8), (1, 2)))
    small_queries = draw_small_queries(jax.random.fold_in(jax.random.fold_in(splits[9], part), 71), part)
    small_keys = draw_small_keys(jax.random.fold_in(jax.random.fold_in(splits[9], part), 71), part)
    small_values = gaussian(part_keys[5], (TOKENS, HS * DH), 1.0, 6.0, ((0, 16),))
    big_readout = gaussian(splits[6], (HB * DH, LAT), (max(HB * DH // 64, 1)) ** -0.5, 0.75, ((0, 2),))
    small_readout = gaussian(splits[7], (HS * DH, LAT), (max(HS * DH // 64, 1)) ** -0.5, 1.5)
    guidance = jnp.clip(jax.random.uniform(part_keys[8], (1,), jnp.float32, 1.0, 4.0), 1.0, 4.0)
    return dict(big_queries=big_queries, big_keys=big_keys, big_values=big_values, small_queries=small_queries, small_keys=small_keys, small_values=small_values, big_readout=big_readout, small_readout=small_readout, guidance=guidance)


def attend_head(operands):
    query_head, key_head, value_head = operands
    scores = jnp.dot(query_head, key_head.T, preferred_element_type=jnp.float32) * (1.0 / math.sqrt(DH))
    row_max = lax.optimization_barrier(jnp.max(scores, axis=1, keepdims=True))
    probs = jnp.exp(scores - row_max)
    totals = lax.optimization_barrier(jnp.sum(probs, axis=1, keepdims=True))
    weights = probs.astype(jnp.bfloat16)
    attended = jnp.dot(weights, value_head, preferred_element_type=jnp.float32) / totals
    return attended.astype(jnp.bfloat16)

def split_model(matrix, heads):
    return jnp.transpose(matrix.reshape(TOKENS, heads, DH), (1, 0, 2))

def run_model(query_all, key_all, value_all, heads):
    outputs = lax.map(attend_head, (split_model(query_all, heads), split_model(key_all, heads), split_model(value_all, heads)))
    return jnp.transpose(outputs, (1, 0, 2)).reshape(TOKENS, heads * DH)

def reference(big_queries, big_keys, big_values, small_queries, small_keys, small_values, big_readout, small_readout, guidance):
    big_attention = run_model(big_queries, big_keys, big_values, HB)
    small_attention = run_model(small_queries, small_keys, small_values, HS)
    big_latent = jnp.dot(big_attention, big_readout, preferred_element_type=jnp.float32)
    small_latent = jnp.dot(small_attention, small_readout, preferred_element_type=jnp.float32)
    blended = big_latent + guidance[0] * (big_latent - small_latent)
    return blended.reshape(TOKENS // 2, 2 * LAT)
```

```python
import functools
import math

import jax
import jax.numpy as jnp
from jax import lax
from jax.experimental import pallas as pl
from jax.experimental.pallas import tpu as pltpu
from jax.sharding import PartitionSpec as P

DH = 128


def split_heads(matrix, blocks, parts):
    rows_here, columns = matrix.shape
    shaped = matrix.reshape(blocks, rows_here // blocks, parts, columns // parts)
    shaped = jnp.transpose(shaped, (0, 2, 1, 3))
    return shaped.reshape(blocks * parts, rows_here // blocks, columns // parts)


def copy_heads(matrix, blocks, parts):
    rows_here, columns = matrix.shape
    shaped = jnp.transpose(matrix.reshape(rows_here, parts, columns // parts), (1, 0, 2))
    shaped = jnp.broadcast_to(shaped[None], (blocks, parts, rows_here, columns // parts))
    return shaped.reshape(blocks * parts, rows_here, columns // parts)


def join_heads(stacked, blocks, parts):
    pieces, rows_here, columns = stacked.shape
    shaped = stacked.reshape(blocks, parts, rows_here, columns)
    shaped = jnp.transpose(shaped, (0, 2, 1, 3))
    return shaped.reshape(blocks * rows_here, parts * columns)


def attend(query_rows, key_rows, value_rows):
    query_count = query_rows.shape[0]
    heads_here = query_rows.shape[1] // DH
    key_count = key_rows.shape[0]
    block_height = math.gcd(query_count, 256)
    block_count = query_count // block_height
    query_blocks = query_rows.reshape(block_count, block_height, heads_here, DH)
    key_split = key_rows.reshape(key_count, heads_here, DH)
    value_split = value_rows.reshape(key_count, heads_here, DH)
    score_scale = 1.0 / math.sqrt(DH)

    def one_block(query_block):
        scores = (
            jnp.einsum("qgd,kgd->gqk", query_block, key_split, preferred_element_type=jnp.float32)
            * score_scale
        )
        row_max = jnp.max(scores, axis=2, keepdims=True)
        probs = jnp.exp(scores - row_max)
        totals = jnp.sum(probs, axis=2, keepdims=True)
        weights = probs.astype(jnp.bfloat16)
        accumulated = jnp.einsum(
            "gqk,kgd->gqd", weights, value_split, preferred_element_type=jnp.float32
        )
        attended = accumulated / totals
        attended = jnp.transpose(attended, (1, 0, 2)).reshape(block_height, heads_here * DH)
        return attended.astype(jnp.bfloat16)

    outputs = lax.map(one_block, query_blocks)
    return outputs.reshape(query_count, heads_here * DH)


def exchanged(
    big_queries,
    big_keys,
    big_values,
    small_queries,
    small_keys,
    small_values,
    big_readout,
    small_readout,
    guidance,
):
    seq_count = lax.axis_size("seq")
    big_heads = big_queries.shape[1] // DH
    big_group = max(big_heads // seq_count, 1)
    big_blocks = max(seq_count // big_heads, 1)
    big_parts = big_heads // big_group
    query_rows = lax.all_to_all(
        split_heads(big_queries, big_blocks, big_parts),
        "seq",
        split_axis=0,
        concat_axis=1,
        tiled=True,
    )[0]
    key_copies, value_copies = (
        lax.all_to_all(
            copy_heads(big_keys, big_blocks, big_parts),
            "seq",
            split_axis=0,
            concat_axis=1,
            tiled=True,
        ),
        lax.all_to_all(
            copy_heads(big_values, big_blocks, big_parts),
            "seq",
            split_axis=0,
            concat_axis=1,
            tiled=True,
        ),
    )
    key_rows = key_copies[0]
    value_rows = value_copies[0]
    big_out = attend(query_rows, key_rows, value_rows)
    big_back = lax.all_to_all(big_out[None], "seq", split_axis=1, concat_axis=0, tiled=True)
    big_attention = join_heads(big_back, big_blocks, big_parts)
    big_partial = jnp.dot(big_attention, big_readout, preferred_element_type=jnp.float32)
    small_heads = small_queries.shape[1] // DH
    small_group = max(small_heads // seq_count, 1)
    small_blocks = max(seq_count // small_heads, 1)
    small_parts = small_heads // small_group
    small_query_rows = lax.all_to_all(
        split_heads(small_queries, small_blocks, small_parts),
        "seq",
        split_axis=0,
        concat_axis=1,
        tiled=True,
    )[0]
    key_copies, value_copies = (
        lax.all_to_all(
            copy_heads(small_keys, small_blocks, small_parts),
            "seq",
            split_axis=0,
            concat_axis=1,
            tiled=True,
        ),
        lax.all_to_all(
            copy_heads(small_values, small_blocks, small_parts),
            "seq",
            split_axis=0,
            concat_axis=1,
            tiled=True,
        ),
    )
    small_key_rows, small_value_rows = (
        lax.all_gather(key_copies[0], "head", axis=0, tiled=True),
        lax.all_gather(value_copies[0], "head", axis=0, tiled=True),
    )
    small_out = attend(small_query_rows, small_key_rows, small_value_rows)
    small_back = lax.all_to_all(small_out[None], "seq", split_axis=1, concat_axis=0, tiled=True)
    small_attention = join_heads(small_back, small_blocks, small_parts)
    small_latent = jnp.dot(small_attention, small_readout, preferred_element_type=jnp.float32)
    weight_value = guidance[0]
    core_index = lax.axis_index("head")
    placed = lax.dynamic_update_slice(
        jnp.zeros_like(big_partial),
        small_latent,
        (core_index * small_latent.shape[0], jnp.zeros((), jnp.int32)),
    )
    blended = lax.psum((1.0 + weight_value) * big_partial - weight_value * placed, "head")
    return blended.reshape(blended.shape[0] // 2, 2 * blended.shape[1])


MESH = pl.DeviceIdType.MESH


def far_first(count):
    return sorted(range(1, count), key=lambda offset: -min(offset, count - offset))


def softmax_parts(query_head, key_head):
    scores = lax.dot_general(
        query_head, key_head, (((1,), (1,)), ((), ())), preferred_element_type=jnp.float32
    ) * (1.0 / math.sqrt(DH))
    row_max = jnp.max(scores, axis=1, keepdims=True)
    probs = jnp.exp(scores - row_max)
    totals = jnp.sum(probs, axis=1, keepdims=True)
    return probs.astype(jnp.bfloat16), totals


def weigh(weights, totals, value_head):
    accumulated = jnp.dot(weights, value_head, preferred_element_type=jnp.float32)
    return (accumulated / totals).astype(jnp.bfloat16)


def fused_kernel(
    n,
    m,
    guidance,
    big_q,
    big_k,
    big_v,
    small_q,
    small_k,
    small_v,
    big_read,
    small_read,
    out,
    all_q,
    all_k,
    all_v,
    few_q,
    few_k,
    few_v,
    read_big,
    read_small,
    weights,
    latent,
    small_part,
    stage,
    arrived,
    own_sem,
    big_send,
    big_recv,
    small_send,
    small_recv,
    back_send,
    back_recv,
):
    group = lax.axis_index("groups")
    me = lax.axis_index("seq")
    core = lax.axis_index("head")
    rows = big_q.shape[0]
    width = all_q.shape[1]
    few_rows = small_q.shape[0]
    few_width = few_q.shape[1]
    heads_here = width // DH
    few_heads = few_width // DH
    lat = big_read.shape[1]
    half = stage.shape[1]
    order = far_first(n)

    def ahead(offset):
        return lax.rem(me + offset, n)

    def behind(offset):
        return lax.rem(me + n - offset, n)

    def window(ref, index, size):
        return ref.at[:, pl.ds(pl.multiple_of(index * size, size), size)]

    def big_land(ref, seq):
        return ref.at[pl.ds(pl.multiple_of(seq * rows, rows), rows), :]

    def few_land(ref, seq, which):
        start = pl.multiple_of((seq * m + which) * few_rows, few_rows)
        return ref.at[pl.ds(start, few_rows), :]

    big_pairs = ((big_k, all_k), (big_q, all_q), (big_v, all_v))
    few_pairs = ((small_k, few_k), (small_q, few_q), (small_v, few_v))

    def big_copy(item, offset, landing):
        source, target = big_pairs[item]
        peer = ahead(offset)
        return pltpu.make_async_remote_copy(
            src_ref=window(source, peer, width),
            dst_ref=big_land(target, landing),
            send_sem=big_send.at[item, offset],
            recv_sem=big_recv.at[item, offset],
            device_id=(group, peer, core),
            device_id_type=MESH,
        )

    def few_copy(item, offset, landing, which):
        source, target = few_pairs[item]
        peer = ahead(offset)
        return pltpu.make_async_remote_copy(
            src_ref=window(source, peer, few_width),
            dst_ref=few_land(target, landing, which),
            send_sem=small_send.at[item, offset],
            recv_sem=small_recv.at[item, offset, which],
            device_id=(group, peer, 0),
            device_id_type=MESH,
        )

    def back_copy(offset, turn, slot_core):
        peer = ahead(offset)
        return pltpu.make_async_remote_copy(
            src_ref=stage.at[peer],
            dst_ref=arrived.at[offset, slot_core],
            send_sem=back_send.at[offset, turn],
            recv_sem=back_recv.at[offset, slot_core],
            device_id=(group, peer, lax.rem(core + turn, m)),
            device_id_type=MESH,
        )

    barrier = pltpu.get_barrier_semaphore()
    for offset in range(n):
        for turn in range(m):
            if offset or turn:
                pl.semaphore_signal(
                    barrier,
                    inc=1,
                    device_id=(group, ahead(offset), lax.rem(core + turn, m)),
                    device_id_type=MESH,
                )

    read_rows = pl.ds(pl.multiple_of(me * width, width), width)
    few_read_rows = pl.ds(pl.multiple_of(me * few_width, few_width), few_width)
    own = [
        pltpu.make_async_copy(
            window(source, me, width), big_land(target, me), own_sem.at[item]
        )
        for item, (source, target) in enumerate(big_pairs)
    ]
    own.append(pltpu.make_async_copy(big_read.at[read_rows, :], read_big, own_sem.at[3]))
    own.append(
        pltpu.make_async_copy(small_read.at[few_read_rows, :], read_small, own_sem.at[4])
    )
    few_own = [
        pltpu.make_async_copy(
            window(source, me, few_width), few_land(target, me, 0), own_sem.at[5 + item]
        )
        for item, (source, target) in enumerate(few_pairs)
    ]
    for copy in own:
        copy.start()

    @pl.when(core == 0)
    def _():
        for copy in few_own:
            copy.start()

    pl.semaphore_wait(barrier, n * m - 1)

    for offset in order:
        for item in range(3):
            few_copy(item, offset, me, core).start()

    @pl.when(core != 0)
    def _():
        for item in range(3):
            few_copy(item, 0, me, core).start()

    for items in ((0, 1), (2,)):
        for offset in order:
            for item in items:
                big_copy(item, offset, me).start()

    for copy in own:
        copy.wait()
    weight_value = guidance[0]
    lanes = lax.broadcasted_iota(jnp.int32, (latent.shape[0] // 2, 2 * lat), 1)

    def paired(attended, readout):
        doubled = jnp.concatenate([readout, readout], axis=1)
        latent[...] = jnp.dot(attended, doubled, preferred_element_type=jnp.float32)
        even = latent[pl.ds(0, latent.shape[0] // 2, stride=2), :]
        odd = latent[pl.ds(1, latent.shape[0] // 2, stride=2), :]
        return jnp.where(lanes < lat, even, odd)

    @pl.when(core == 0)
    def _():
        for copy in few_own:
            copy.wait()
        for which in range(m):
            for offset in range(n):
                if offset or which:
                    for item in range(3):
                        few_copy(item, offset, behind(offset), which).wait_recv()
        pieces = []
        for head in range(few_heads):
            columns = slice(head * DH, (head + 1) * DH)
            probs, totals = softmax_parts(few_q[:, columns], few_k[:, columns])
            pieces.append(weigh(probs, totals, few_v[:, columns]))
        attended = pieces[0] if few_heads == 1 else jnp.concatenate(pieces, axis=1)
        small_part[...] = weight_value * paired(attended, read_small[...])

    @pl.when(core != 0)
    def _():
        small_part[...] = jnp.zeros_like(small_part)

    for offset in order:
        for item in (0, 1):
            big_copy(item, offset, behind(offset)).wait_recv()
    totals_of = []
    for head in range(heads_here):
        columns = slice(head * DH, (head + 1) * DH)
        probs, totals = softmax_parts(all_q[:, columns], all_k[:, columns])
        weights[head] = probs
        totals_of.append(totals)
    for offset in order:
        big_copy(2, offset, behind(offset)).wait_recv()
    pieces = [
        weigh(weights[head], totals_of[head], all_v[:, head * DH : (head + 1) * DH])
        for head in range(heads_here)
    ]
    attended = pieces[0] if heads_here == 1 else jnp.concatenate(pieces, axis=1)
    term = (1.0 + weight_value) * paired(attended, read_big[...]) - small_part[...]
    stage[...] = term.reshape(n, half, 2 * lat)
    arrived[0, core] = stage[me]

    for offset in order + [0]:
        for turn in range(m):
            if offset or turn:
                back_copy(offset, turn, core).start()
    for offset in range(n):
        for slot_core in range(m):
            if offset:
                back_copy(offset, 0, slot_core).wait_recv()
    for turn in range(1, m):
        back_copy(0, turn, lax.rem(core + turn, m)).wait_recv()
    out[...] = jnp.sum(arrived[...].reshape(n * m, half, 2 * lat), axis=0)

    for offset in order:
        for item in range(3):
            few_copy(item, offset, me, core).wait_send()
            big_copy(item, offset, me).wait_send()

    @pl.when(core != 0)
    def _():
        for item in range(3):
            few_copy(item, 0, me, core).wait_send()

    for offset in order + [0]:
        for turn in range(m):
            if offset or turn:
                back_copy(offset, turn, core).wait_send()


def fused(
    n,
    m,
    big_queries,
    big_keys,
    big_values,
    small_queries,
    small_keys,
    small_values,
    big_readout,
    small_readout,
    guidance,
):
    rows, columns = big_queries.shape
    few_rows, few_columns = small_queries.shape
    width, few_width = columns // n, few_columns // n
    tokens = rows * n
    lat = big_readout.shape[1]
    half = rows // 2
    kind = jnp.bfloat16
    dma = pltpu.SemaphoreType.DMA
    return pl.pallas_call(
        functools.partial(fused_kernel, n, m),
        out_shape=jax.ShapeDtypeStruct((half, 2 * lat), jnp.float32),
        in_specs=[pl.BlockSpec(memory_space=pltpu.SMEM)]
        + [pl.BlockSpec(memory_space=pl.ANY)] * 8,
        out_specs=pl.BlockSpec(memory_space=pltpu.VMEM),
        scratch_shapes=[
            pltpu.VMEM((tokens, width), kind),
            pltpu.VMEM((tokens, width), kind),
            pltpu.VMEM((tokens, width), kind),
            pltpu.VMEM((tokens, few_width), kind),
            pltpu.VMEM((tokens, few_width), kind),
            pltpu.VMEM((tokens, few_width), kind),
            pltpu.VMEM((width, lat), kind),
            pltpu.VMEM((few_width, lat), kind),
            pltpu.VMEM((width // DH, tokens, tokens), kind),
            pltpu.VMEM((tokens, 2 * lat), jnp.float32),
            pltpu.VMEM((tokens // 2, 2 * lat), jnp.float32),
            pltpu.VMEM((n, half, 2 * lat), jnp.float32),
            pltpu.VMEM((n, m, half, 2 * lat), jnp.float32),
            dma((8,)),
            dma((3, n)),
            dma((3, n)),
            dma((3, n)),
            dma((3, n, m)),
            dma((n, m)),
            dma((n, m)),
        ],
        compiler_params=pltpu.CompilerParams(collective_id=0, has_side_effects=True),
        name="fused_window",
    )(
        guidance,
        big_queries,
        big_keys,
        big_values,
        small_queries,
        small_keys,
        small_values,
        big_readout,
        small_readout,
    )


def fits(n, m, big_queries, small_queries, lat):
    rows, columns = big_queries.shape
    few_rows, few_columns = small_queries.shape
    return (
        n > 1
        and m > 1
        and n * rows <= 512
        and columns % (n * DH) == 0
        and few_columns % (n * DH) == 0
        and rows == m * few_rows
        and few_rows % 16 == 0
        and 2 * lat == 128
    )


def shards(*arguments):
    n, m = lax.axis_size("seq"), lax.axis_size("head")
    if fits(n, m, arguments[0], arguments[3], arguments[6].shape[1]):
        return fused(n, m, *arguments)
    return exchanged(*arguments)


def solution(mesh):
    placed = (
        P(("groups", "seq"), "head"),
        P(("groups", "seq"), "head"),
        P(("groups", "seq"), "head"),
        P(("groups", "seq", "head"), None),
        P(("groups", "seq", "head"), None),
        P(("groups", "seq", "head"), None),
        P("head", None),
        P(),
        P("groups"),
    )
    return jax.shard_map(
        shards, mesh=mesh, in_specs=placed, out_specs=P(("groups", "seq"), None), check_vma=False
    )
```

```python
import functools
import math

import jax
import jax.numpy as jnp
from jax import lax
from jax.experimental import pallas as pl
from jax.experimental.pallas import tpu as pltpu
from jax.sharding import PartitionSpec as P

DH = 128


def split_heads(matrix, blocks, parts):
    rows_here, columns = matrix.shape
    shaped = matrix.reshape(blocks, rows_here // blocks, parts, columns // parts)
    shaped = jnp.transpose(shaped, (0, 2, 1, 3))
    return shaped.reshape(blocks * parts, rows_here // blocks, columns // parts)


def copy_heads(matrix, blocks, parts):
    rows_here, columns = matrix.shape
    shaped = jnp.transpose(matrix.reshape(rows_here, parts, columns // parts), (1, 0, 2))
    shaped = jnp.broadcast_to(shaped[None], (blocks, parts, rows_here, columns // parts))
    return shaped.reshape(blocks * parts, rows_here, columns // parts)


def join_heads(stacked, blocks, parts):
    pieces, rows_here, columns = stacked.shape
    shaped = stacked.reshape(blocks, parts, rows_here, columns)
    shaped = jnp.transpose(shaped, (0, 2, 1, 3))
    return shaped.reshape(blocks * rows_here, parts * columns)


def attend(query_rows, key_rows, value_rows):
    query_count = query_rows.shape[0]
    heads_here = query_rows.shape[1] // DH
    key_count = key_rows.shape[0]
    block_height = math.gcd(query_count, 256)
    block_count = query_count // block_height
    query_blocks = query_rows.reshape(block_count, block_height, heads_here, DH)
    key_split = key_rows.reshape(key_count, heads_here, DH)
    value_split = value_rows.reshape(key_count, heads_here, DH)
    score_scale = 1.0 / math.sqrt(DH)

    def one_block(query_block):
        scores = (
            jnp.einsum("qgd,kgd->gqk", query_block, key_split, preferred_element_type=jnp.float32)
            * score_scale
        )
        row_max = jnp.max(scores, axis=2, keepdims=True)
        probs = jnp.exp(scores - row_max)
        totals = jnp.sum(probs, axis=2, keepdims=True)
        weights = probs.astype(jnp.bfloat16)
        accumulated = jnp.einsum(
            "gqk,kgd->gqd", weights, value_split, preferred_element_type=jnp.float32
        )
        attended = accumulated / totals
        attended = jnp.transpose(attended, (1, 0, 2)).reshape(block_height, heads_here * DH)
        return attended.astype(jnp.bfloat16)

    outputs = lax.map(one_block, query_blocks)
    return outputs.reshape(query_count, heads_here * DH)


def exchanged(
    big_queries,
    big_keys,
    big_values,
    small_queries,
    small_keys,
    small_values,
    big_readout,
    small_readout,
    guidance,
):
    seq_count = lax.axis_size("seq")
    big_heads = big_queries.shape[1] // DH
    big_group = max(big_heads // seq_count, 1)
    big_blocks = max(seq_count // big_heads, 1)
    big_parts = big_heads // big_group
    query_rows = lax.all_to_all(
        split_heads(big_queries, big_blocks, big_parts),
        "seq",
        split_axis=0,
        concat_axis=1,
        tiled=True,
    )[0]
    key_copies, value_copies = (
        lax.all_to_all(
            copy_heads(big_keys, big_blocks, big_parts),
            "seq",
            split_axis=0,
            concat_axis=1,
            tiled=True,
        ),
        lax.all_to_all(
            copy_heads(big_values, big_blocks, big_parts),
            "seq",
            split_axis=0,
            concat_axis=1,
            tiled=True,
        ),
    )
    key_rows = key_copies[0]
    value_rows = value_copies[0]
    big_out = attend(query_rows, key_rows, value_rows)
    big_back = lax.all_to_all(big_out[None], "seq", split_axis=1, concat_axis=0, tiled=True)
    big_attention = join_heads(big_back, big_blocks, big_parts)
    big_partial = jnp.dot(big_attention, big_readout, preferred_element_type=jnp.float32)
    small_heads = small_queries.shape[1] // DH
    small_group = max(small_heads // seq_count, 1)
    small_blocks = max(seq_count // small_heads, 1)
    small_parts = small_heads // small_group
    small_query_rows = lax.all_to_all(
        split_heads(small_queries, small_blocks, small_parts),
        "seq",
        split_axis=0,
        concat_axis=1,
        tiled=True,
    )[0]
    key_copies, value_copies = (
        lax.all_to_all(
            copy_heads(small_keys, small_blocks, small_parts),
            "seq",
            split_axis=0,
            concat_axis=1,
            tiled=True,
        ),
        lax.all_to_all(
            copy_heads(small_values, small_blocks, small_parts),
            "seq",
            split_axis=0,
            concat_axis=1,
            tiled=True,
        ),
    )
    small_key_rows, small_value_rows = (
        lax.all_gather(key_copies[0], "head", axis=0, tiled=True),
        lax.all_gather(value_copies[0], "head", axis=0, tiled=True),
    )
    small_out = attend(small_query_rows, small_key_rows, small_value_rows)
    small_back = lax.all_to_all(small_out[None], "seq", split_axis=1, concat_axis=0, tiled=True)
    small_attention = join_heads(small_back, small_blocks, small_parts)
    small_latent = jnp.dot(small_attention, small_readout, preferred_element_type=jnp.float32)
    weight_value = guidance[0]
    core_index = lax.axis_index("head")
    placed = lax.dynamic_update_slice(
        jnp.zeros_like(big_partial),
        small_latent,
        (core_index * small_latent.shape[0], jnp.zeros((), jnp.int32)),
    )
    blended = lax.psum((1.0 + weight_value) * big_partial - weight_value * placed, "head")
    return blended.reshape(blended.shape[0] // 2, 2 * blended.shape[1])


MESH = pl.DeviceIdType.MESH


def far_first(count):
    return sorted(range(1, count), key=lambda offset: -min(offset, count - offset))


def softmax_parts(query_head, key_head):
    scores = lax.dot_general(
        query_head, key_head, (((1,), (1,)), ((), ())), preferred_element_type=jnp.float32
    ) * (1.0 / math.sqrt(DH))
    row_max = jnp.max(scores, axis=1, keepdims=True)
    probs = jnp.exp(scores - row_max)
    totals = jnp.sum(probs, axis=1, keepdims=True)
    return probs.astype(jnp.bfloat16), totals


def weigh(weights, totals, value_head):
    accumulated = jnp.dot(weights, value_head, preferred_element_type=jnp.float32)
    return (accumulated / totals).astype(jnp.bfloat16)


def fused_kernel(
    n,
    m,
    guidance,
    big_q,
    big_k,
    big_v,
    small_q,
    small_k,
    small_v,
    big_read,
    small_read,
    out,
    all_q,
    all_k,
    all_v,
    few_q,
    few_k,
    few_v,
    read_big,
    read_small,
    weights,
    latent,
    small_part,
    stage,
    arrived,
    guide,
    own_sem,
    big_send,
    big_recv,
    small_send,
    small_recv,
    back_send,
    back_recv,
):
    group = lax.axis_index("groups")
    me = lax.axis_index("seq")
    core = lax.axis_index("head")
    rows = big_q.shape[0]
    width = all_q.shape[1]
    few_rows = small_q.shape[0]
    few_width = few_q.shape[1]
    heads_here = width // DH
    few_heads = few_width // DH
    lat = big_read.shape[0]
    half = stage.shape[1]
    order = far_first(n)

    def ahead(offset):
        return lax.rem(me + offset, n)

    def behind(offset):
        return lax.rem(me + n - offset, n)

    def window(ref, index, size):
        return ref.at[:, pl.ds(pl.multiple_of(index * size, size), size)]

    def big_land(ref, seq):
        return ref.at[pl.ds(pl.multiple_of(seq * rows, rows), rows), :]

    def few_land(ref, seq, which):
        start = pl.multiple_of((seq * m + which) * few_rows, few_rows)
        return ref.at[pl.ds(start, few_rows), :]

    big_pairs = ((big_k, all_k), (big_q, all_q), (big_v, all_v))
    few_pairs = ((small_k, few_k), (small_q, few_q), (small_v, few_v))

    def big_copy(item, offset, landing):
        source, target = big_pairs[item]
        peer = ahead(offset)
        return pltpu.make_async_remote_copy(
            src_ref=window(source, peer, width),
            dst_ref=big_land(target, landing),
            send_sem=big_send.at[item, offset],
            recv_sem=big_recv.at[item, offset],
            device_id=(group, peer, core),
            device_id_type=MESH,
        )

    def few_copy(item, offset, landing, which):
        source, target = few_pairs[item]
        peer = ahead(offset)
        return pltpu.make_async_remote_copy(
            src_ref=window(source, peer, few_width),
            dst_ref=few_land(target, landing, which),
            send_sem=small_send.at[item, offset],
            recv_sem=small_recv.at[item, offset, which],
            device_id=(group, peer, 0),
            device_id_type=MESH,
        )

    def back_copy(offset, turn, slot_core):
        peer = ahead(offset)
        return pltpu.make_async_remote_copy(
            src_ref=stage.at[peer],
            dst_ref=arrived.at[offset, slot_core],
            send_sem=back_send.at[offset, turn],
            recv_sem=back_recv.at[offset, slot_core],
            device_id=(group, peer, lax.rem(core + turn, m)),
            device_id_type=MESH,
        )

    barrier = pltpu.get_barrier_semaphore()
    for offset in range(n):
        for turn in range(m):
            if offset or turn:
                pl.semaphore_signal(
                    barrier,
                    inc=1,
                    device_id=(group, ahead(offset), lax.rem(core + turn, m)),
                    device_id_type=MESH,
                )

    read_rows = pl.ds(pl.multiple_of(me * width, width), width)
    few_read_rows = pl.ds(pl.multiple_of(me * few_width, few_width), few_width)
    own = [
        pltpu.make_async_copy(
            window(source, me, width), big_land(target, me), own_sem.at[item]
        )
        for item, (source, target) in enumerate(big_pairs)
    ]
    own.append(pltpu.make_async_copy(big_read.at[:, read_rows], read_big, own_sem.at[3]))
    own.append(
        pltpu.make_async_copy(small_read.at[:, few_read_rows], read_small, own_sem.at[4])
    )
    own.append(pltpu.make_async_copy(guidance, guide, own_sem.at[8]))
    few_own = [
        pltpu.make_async_copy(
            window(source, me, few_width), few_land(target, me, 0), own_sem.at[5 + item]
        )
        for item, (source, target) in enumerate(few_pairs)
    ]
    for copy in own:
        copy.start()

    @pl.when(core == 0)
    def _():
        for copy in few_own:
            copy.start()

    pl.semaphore_wait(barrier, n * m - 1)

    for offset in order:
        for item in range(3):
            few_copy(item, offset, me, core).start()

    @pl.when(core != 0)
    def _():
        for item in range(3):
            few_copy(item, 0, me, core).start()

    for items in ((0, 1), (2,)):
        for offset in order:
            for item in items:
                big_copy(item, offset, me).start()

    for copy in own:
        copy.wait()
    weight_value = guide[0]
    lanes = lax.broadcasted_iota(jnp.int32, (latent.shape[0] // 2, 2 * lat), 1)

    def paired(attended, readout):
        doubled = jnp.concatenate([readout, readout], axis=0)
        latent[...] = lax.dot_general(
            attended, doubled, (((1,), (1,)), ((), ())), preferred_element_type=jnp.float32
        )
        even = latent[pl.ds(0, latent.shape[0] // 2, stride=2), :]
        odd = latent[pl.ds(1, latent.shape[0] // 2, stride=2), :]
        return jnp.where(lanes < lat, even, odd)

    @pl.when(core == 0)
    def _():
        for copy in few_own:
            copy.wait()
        for which in range(m):
            for offset in range(n):
                if offset or which:
                    for item in range(3):
                        few_copy(item, offset, behind(offset), which).wait_recv()
        pieces = []
        for head in range(few_heads):
            columns = slice(head * DH, (head + 1) * DH)
            probs, totals = softmax_parts(few_q[:, columns], few_k[:, columns])
            pieces.append(weigh(probs, totals, few_v[:, columns]))
        attended = pieces[0] if few_heads == 1 else jnp.concatenate(pieces, axis=1)
        small_part[...] = weight_value * paired(attended, read_small[...])

    @pl.when(core != 0)
    def _():
        small_part[...] = jnp.zeros_like(small_part)

    for offset in order:
        for item in (0, 1):
            big_copy(item, offset, behind(offset)).wait_recv()
    totals_of = []
    for head in range(heads_here):
        columns = slice(head * DH, (head + 1) * DH)
        probs, totals = softmax_parts(all_q[:, columns], all_k[:, columns])
        weights[head] = probs
        totals_of.append(totals)
    for offset in order:
        big_copy(2, offset, behind(offset)).wait_recv()
    pieces = [
        weigh(weights[head], totals_of[head], all_v[:, head * DH : (head + 1) * DH])
        for head in range(heads_here)
    ]
    attended = pieces[0] if heads_here == 1 else jnp.concatenate(pieces, axis=1)
    term = (1.0 + weight_value) * paired(attended, read_big[...]) - small_part[...]
    stage[...] = term.reshape(n, half, 2 * lat)
    arrived[0, core] = stage[me]

    for offset in order + [0]:
        for turn in range(m):
            if offset or turn:
                back_copy(offset, turn, core).start()
    for offset in range(n):
        for slot_core in range(m):
            if offset:
                back_copy(offset, 0, slot_core).wait_recv()
    for turn in range(1, m):
        back_copy(0, turn, lax.rem(core + turn, m)).wait_recv()
    out[...] = jnp.sum(arrived[...].reshape(n * m, half, 2 * lat), axis=0)

    for offset in order:
        for item in range(3):
            few_copy(item, offset, me, core).wait_send()
            big_copy(item, offset, me).wait_send()

    @pl.when(core != 0)
    def _():
        for item in range(3):
            few_copy(item, 0, me, core).wait_send()

    for offset in order + [0]:
        for turn in range(m):
            if offset or turn:
                back_copy(offset, turn, core).wait_send()


def fused(
    n,
    m,
    big_queries,
    big_keys,
    big_values,
    small_queries,
    small_keys,
    small_values,
    big_readout,
    small_readout,
    guidance,
):
    rows, columns = big_queries.shape
    few_rows, few_columns = small_queries.shape
    width, few_width = columns // n, few_columns // n
    tokens = rows * n
    lat = big_readout.shape[1]
    half = rows // 2
    kind = jnp.bfloat16
    dma = pltpu.SemaphoreType.DMA
    return pl.pallas_call(
        functools.partial(fused_kernel, n, m),
        out_shape=pltpu.VMEM((half, 2 * lat), jnp.float32),
        in_specs=[pl.BlockSpec(memory_space=pl.ANY)] * 9,
        out_specs=pl.BlockSpec(memory_space=pltpu.VMEM),
        scratch_shapes=[
            pltpu.VMEM((tokens, width), kind),
            pltpu.VMEM((tokens, width), kind),
            pltpu.VMEM((tokens, width), kind),
            pltpu.VMEM((tokens, few_width), kind),
            pltpu.VMEM((tokens, few_width), kind),
            pltpu.VMEM((tokens, few_width), kind),
            pltpu.VMEM((lat, width), kind),
            pltpu.VMEM((lat, few_width), kind),
            pltpu.VMEM((width // DH, tokens, tokens), kind),
            pltpu.VMEM((tokens, 2 * lat), jnp.float32),
            pltpu.VMEM((tokens // 2, 2 * lat), jnp.float32),
            pltpu.VMEM((n, half, 2 * lat), jnp.float32),
            pltpu.VMEM((n, m, half, 2 * lat), jnp.float32),
            pltpu.SMEM((1,), jnp.float32),
            dma((9,)),
            dma((3, n)),
            dma((3, n)),
            dma((3, n)),
            dma((3, n, m)),
            dma((n, m)),
            dma((n, m)),
        ],
        compiler_params=pltpu.CompilerParams(collective_id=0, has_side_effects=True),
        name="fused_window",
    )(
        guidance,
        big_queries,
        big_keys,
        big_values,
        small_queries,
        small_keys,
        small_values,
        big_readout.T,
        small_readout.T,
    )


def fits(n, m, big_queries, small_queries, lat):
    rows, columns = big_queries.shape
    few_rows, few_columns = small_queries.shape
    return (
        n > 1
        and m > 1
        and n * rows <= 512
        and columns % (n * DH) == 0
        and few_columns % (n * DH) == 0
        and rows == m * few_rows
        and few_rows % 16 == 0
        and 2 * lat == 128
    )


def shards(*arguments):
    n, m = lax.axis_size("seq"), lax.axis_size("head")
    if fits(n, m, arguments[0], arguments[3], arguments[6].shape[1]):
        return fused(n, m, *arguments)
    return exchanged(*arguments)


def solution(mesh):
    placed = (
        P(("groups", "seq"), "head"),
        P(("groups", "seq"), "head"),
        P(("groups", "seq"), "head"),
        P(("groups", "seq", "head"), None),
        P(("groups", "seq", "head"), None),
        P(("groups", "seq", "head"), None),
        P("head", None),
        P(),
        P("groups"),
    )
    return jax.shard_map(
        shards, mesh=mesh, in_specs=placed, out_specs=P(("groups", "seq"), None), check_vma=False
    )
```
